32 devices in a mesh: grp: 2 (over x), sec: 8 (over z, y), head: 2 (over core).
Axes of the slice: x: 2, y: 2, z: 4, core: 2. Of those that a mesh axis runs over, the one named last changes fastest.
Arguments:
- patches: bfloat16 [4, 64, 1408], P('grp', 'head'), parts along dimension 0, may hold values from -6 to 6
- stale_kv: bfloat16 [16, 2, 512, 1408], P(('grp', 'sec'), None, None, 'head'), parts along dimension 0, as said below
- qkv_weight: bfloat16 [8, 3, 1408, 1408], P('sec', None, None, 'head'), may hold values from -0.15625 to 0.15625
- out_weight: bfloat16 [8, 1408, 1408], P('sec', 'head'), may hold values from -0.15625 to 0.15625
- skip_joined_weight: bfloat16 [8, 2816, 1408], P('sec'), may hold values from -0.109375 to 0.109375
- qk_gain: bfloat16 [8, 2, 1408], P('sec', None, 'head'), may hold values from 0.5 to 1.5
- order: int32 [16], P('grp'), parts along dimension 0, may hold values from 0 to 7, each once
- tile_index: int32 [2], P('grp'), parts along dimension 0, may hold values from 0 to 15
Outputs:
- section_out: bfloat16 [8, 4, 64, 1408], P('sec', 'grp', 'head'), parts along dimension 1
The draws below stay inside these ranges and needn't reach their ends.
There are 2 independent parts, one for each index of `grp`. The reference program is written for one: setup_inputs(seed, part) draws one part's arguments, and reference() takes and returns one part's arrays. A program takes and returns all parts, laid end to end along the dimension named above; an argument that names none is the same for every part. Nothing has to cross between parts.
Inputs may be any that keep to these rules, and one draw needn't show every extreme that they name: The first 2 entries name the slots of the patches, in the order of patches; all entries are distinct. `stale_kv`: in the key half, the 88 entries of each head of each row have a root mean square of at most 1.51.
All inputs are finite; a program needn't handle non-finite values.
Results may differ from the reference program's by a relative error of at most 0.018.
Values may be sent and summed in bfloat16 or wider, within the bound.
No kernel may reach another device: no remote copies, remote signals or barrier semaphores. Data moves between devices by JAX's collectives and lax.ppermute only.
A program may use at most 64 MiB of HBM per device.

```python
import math
import jax
import jax.numpy as jnp
from jax import lax

D = 1408
HEADS = 16
HEAD_DIM = 88
PROWS = 64
PATCHES = 2
PATCH_SLOTS = 8
IMG_TILES = 16
TILE = 512
SECTIONS = 8


def draw_stale_kv(key, part):
    key_keys = jax.random.fold_in(key, 11)
    key_vals = jax.random.fold_in(key, 12)
    key_scale = jax.random.fold_in(key, 13)
    shape = (SECTIONS, TILE, HEADS, HEAD_DIM)
    raw = jax.random.normal(key_keys, shape, jnp.float32)
    scale_factors = jax.random.uniform(key_scale, (SECTIONS, TILE, HEADS, 1), jnp.float32, 0.5, 1.5)
    values = jax.random.normal(key_vals, (SECTIONS, TILE, D), jnp.float32)
    squares = jnp.mean(raw * raw, axis=-1, keepdims=True)
    keys_out = raw / jnp.sqrt(squares + 1e-06) * scale_factors
    stacked = jnp.stack([keys_out.reshape(SECTIONS, TILE, D), values], axis=1)
    return stacked.astype(jnp.bfloat16)


def level_of(stream_key, shape, shards, low, high):
    factor_of, own = 1.0, jax.random.fold_in(stream_key, 6)
    for dim, parts in shards:
        heights = jnp.exp(jax.random.uniform(jax.random.fold_in(own, dim), (parts,), jnp.float32, low / len(shards), high / len(shards)))
        factor_of = factor_of * jnp.repeat(heights, shape[dim] // parts).reshape([-1 if axis == dim else 1 for axis in range(len(shape))])
    return factor_of


def gaussian(own_key, dims, scale, most, split=(), kind=jnp.bfloat16):
    array = jax.random.normal(own_key, dims, jnp.float32) * scale
    if len(split) > 0:
        array = level_of(own_key, dims, split, -0.22, 0.18) * array
    return jnp.clip(array, min=-most, max=most).astype(kind)


def setup_inputs(seed: int = 0, part: int = 0) -> dict:
    splits = jax.random.split(jax.random.key(seed), 9)
    own_keys = jax.random.split(jax.random.fold_in(splits[8], part), 9)
    return {
        "patches": gaussian(own_keys[0], (PATCHES, PROWS, D), 1.0, 6.0, ((1, 2),)),
        "stale_kv": draw_stale_kv(jax.random.fold_in(jax.random.fold_in(splits[8], part), 71), part),
        "qkv_weight": gaussian(splits[2], (SECTIONS, 3, D, D), D ** -0.5, 0.15625, ((0, 8), (3, 2))),
        "out_weight": gaussian(splits[3], (SECTIONS, D, D), D ** -0.5, 0.15625, ((0, 8), (1, 2))),
        "skip_joined_weight": gaussian(splits[4], (SECTIONS, 2 * D, D), (2 * D) ** -0.5, 0.109375, ((0, 8),)),
        "qk_gain": jnp.clip(1.0 + 0.1 * jax.random.normal(splits[5], (SECTIONS, 2, D), jnp.float32), 0.5, 1.5).astype(jnp.bfloat16),
        "order": jax.random.permutation(own_keys[6], PATCH_SLOTS).astype(jnp.int32),
        "tile_index": jax.random.randint(own_keys[7], (1,), 0, IMG_TILES).astype(jnp.int32),
    }


EPSILON = 1e-06

def layer_norm(tensor):
    average = lax.optimization_barrier(jnp.mean(tensor, axis=-1, keepdims=True))
    centred = tensor - average
    variance = lax.optimization_barrier(jnp.mean(centred * centred, axis=-1, keepdims=True))
    return centred / jnp.sqrt(variance + EPSILON)

def rotate(tensor, position):
    half_width = tensor.shape[-1] // 2
    inverse = 10000.0 ** (-jnp.arange(half_width, dtype=jnp.float32) / half_width)
    angles = position[:, None] * inverse[None, :]
    cos_table = jnp.cos(angles)[:, None, :]
    sin_table = jnp.sin(angles)[:, None, :]
    leading = tensor[..., :half_width]
    trailing_half = tensor[..., half_width:]
    return jnp.concatenate([leading * cos_table - trailing_half * sin_table, leading * sin_table + trailing_half * cos_table], axis=-1)

def head_norm(projected, gain, position):
    row_count = projected.shape[0]
    heads_here = projected.shape[-1] // HEAD_DIM
    shaped = projected.reshape(row_count, heads_here, HEAD_DIM)
    scaled = layer_norm(shaped) * gain.astype(jnp.float32).reshape(heads_here, HEAD_DIM)
    return rotate(scaled, position).reshape(row_count, heads_here * HEAD_DIM).astype(jnp.bfloat16)

def attention_result(query_rot, key_cache, value_cache):
    row_count = query_rot.shape[0]
    heads_here = query_rot.shape[1] // HEAD_DIM
    query = query_rot.reshape(row_count, heads_here, HEAD_DIM).astype(jnp.float32)
    key_heads = key_cache.reshape(key_cache.shape[0], heads_here, HEAD_DIM).astype(jnp.float32)
    value_heads = value_cache.reshape(value_cache.shape[0], heads_here, HEAD_DIM).astype(jnp.float32)
    scores = jnp.einsum('qhd,khd->hqk', query, key_heads) / math.sqrt(HEAD_DIM)
    expd = jnp.exp(scores)
    weights = (expd / lax.optimization_barrier(jnp.sum(expd, axis=-1, keepdims=True))).astype(jnp.bfloat16)
    mixed = jnp.einsum('hqk,khd->qhd', weights.astype(jnp.float32), value_heads)
    return mixed.reshape(row_count, heads_here * HEAD_DIM).astype(jnp.bfloat16)

def reference(patches, stale_kv, qkv_weight, out_weight, skip_joined_weight, qk_gain, order, tile_index):
    sections = stale_kv.shape[0]
    half_count = sections // 2
    patch_count = patches.shape[0]
    patch_rows = patches.shape[1]
    tile_rows = stale_kv.shape[2]
    row_ids = jnp.arange(patch_rows, dtype=jnp.int32)
    finished = jnp.zeros((sections, patch_count, patch_rows, patches.shape[2]), jnp.bfloat16)
    for section in range(sections):
        key_cache = stale_kv[section, 0]
        value_cache = stale_kv[section, 1]
        produced_list = []
        for patch_idx in range(patch_count):
            source = patches[patch_idx] if section == 0 else finished[section - 1, patch_idx]
            if section >= half_count:
                skip_in = finished[sections - 1 - section, patch_idx]
                joined = jnp.concatenate([source, skip_in], axis=-1)
                mixed = jnp.dot(joined, skip_joined_weight[section], preferred_element_type=jnp.float32)
                residual = layer_norm(mixed).astype(jnp.bfloat16)
            else:
                residual = source
            normed = layer_norm(residual.astype(jnp.float32)).astype(jnp.bfloat16)
            query = jnp.dot(normed, qkv_weight[section, 0], preferred_element_type=jnp.float32)
            key_new = jnp.dot(normed, qkv_weight[section, 1], preferred_element_type=jnp.float32)
            value_raw = jnp.dot(normed, qkv_weight[section, 2], preferred_element_type=jnp.float32)
            row_start = (order[patch_idx] * patch_rows).astype(jnp.int32)
            position = (tile_index[0] * tile_rows + row_start + row_ids).astype(jnp.float32)
            query_rot = head_norm(query, qk_gain[section, 0], position)
            key_rot = head_norm(key_new, qk_gain[section, 1], position)
            value_new = value_raw.astype(jnp.bfloat16)
            key_cache = lax.dynamic_update_slice_in_dim(key_cache, key_rot, row_start, 0)
            value_cache = lax.dynamic_update_slice_in_dim(value_cache, value_new, row_start, 0)
            attended = attention_result(query_rot, key_cache, value_cache)
            update = jnp.dot(attended, out_weight[section], preferred_element_type=jnp.float32)
            produced_list.append((residual.astype(jnp.float32) + update).astype(jnp.bfloat16))
        finished = finished.at[section].set(jnp.stack(produced_list))
    return finished
```

```python
import math

import jax
import jax.numpy as jnp
from jax import lax
from jax.experimental import pallas as pl
from jax.experimental.pallas import tpu as pltpu
from jax.sharding import PartitionSpec as P

HEAD_DIM = 88
HALF = HEAD_DIM // 2
LANES = 128
EPSILON = 1e-06
MASKED = -1e30

VM = pl.BlockSpec(memory_space=pltpu.VMEM)
ANY = pl.BlockSpec(memory_space=pl.ANY)


def windows(width):
    found = []
    for head in range(width // HEAD_DIM):
        first = head * HEAD_DIM
        low = first // LANES * LANES
        high = -(-(first + HEAD_DIM) // LANES) * LANES
        found.append((first, low, high - low))
    return found


def norm_rows(value):
    mean = jnp.mean(value, axis=-1, keepdims=True)
    centred = value - mean
    variance = jnp.mean(centred * centred, axis=-1, keepdims=True)
    return centred / jnp.sqrt(variance + EPSILON)


def params(mib):
    return pltpu.CompilerParams(vmem_limit_bytes=mib << 20)


def in_hbm(value):
    return pltpu.with_memory_space_constraint(value, pltpu.HBM)


def load_first(stale, wqkv, wout, cosine, sine, gains):
    rows = cosine.shape[0]
    width = wqkv.shape[2]
    padded = -(-width // LANES) * LANES

    def kernel(kv_ref, w_ref, o_ref, cos_ref, sin_ref, gain_ref, kv_out, w_out, o_out, tab_out, sems):
        copies = [
            pltpu.make_async_copy(w_ref, w_out, sems.at[0]),
            pltpu.make_async_copy(kv_ref, kv_out, sems.at[1]),
            pltpu.make_async_copy(o_ref, o_out, sems.at[2]),
        ]
        for copy in copies:
            copy.start()
        lane = lax.broadcasted_iota(jnp.int32, (rows, LANES), 1)
        first = lane < HALF
        inside = lane < HEAD_DIM
        cos_base = jnp.where(inside, cos_ref[...], 0.0)
        back = jnp.where(first, -sin_ref[...], 0.0)
        forth = jnp.where(inside & ~first, sin_ref[...], 0.0)
        zero = jnp.zeros((rows, LANES), jnp.float32)
        for which in range(2):
            tab_out[3 * which] = jnp.zeros((rows, padded), jnp.float32)
            tab_out[3 * which + 1] = jnp.zeros((rows, padded), jnp.float32)
            tab_out[3 * which + 2] = jnp.zeros((rows, padded), jnp.float32)
        for start, low, span in windows(width):
            shift = start - low
            span_at = pl.ds(low, span)
            for slot, base in enumerate((cos_base, back, forth)):
                wide = base if span == LANES else jnp.concatenate([base, zero], axis=1)
                moved = pltpu.roll(wide, shift, 1) if shift else wide
                for which in range(2):
                    gain = gain_ref[which : which + 1, span_at]
                    if slot == 1:
                        gain = pltpu.roll(jnp.broadcast_to(gain, (8, span)), span - HALF, 1)[:1]
                    if slot == 2:
                        gain = pltpu.roll(jnp.broadcast_to(gain, (8, span)), HALF, 1)[:1]
                    tab_out[3 * which + slot, :, span_at] += moved * gain
        for copy in copies:
            copy.wait()

    return pl.pallas_call(
        kernel,
        out_shape=(
            pltpu.VMEM(stale.shape, stale.dtype),
            pltpu.VMEM(wqkv.shape, wqkv.dtype),
            pltpu.VMEM(wout.shape, wout.dtype),
            pltpu.VMEM((6, rows, padded), jnp.float32),
        ),
        in_specs=[ANY, ANY, ANY, VM, VM, VM],
        out_specs=(VM, VM, VM, VM),
        scratch_shapes=[pltpu.SemaphoreType.DMA((3,))],
        compiler_params=params(8),
        name="load_first",
    )(in_hbm(stale), in_hbm(wqkv), in_hbm(wout), cosine, sine, gains)


def load_skip(wskip, after):
    def kernel(w_ref, after_ref, w_out, sem):
        copy = pltpu.make_async_copy(w_ref, w_out, sem)
        copy.start()
        copy.wait()

    return pl.pallas_call(
        kernel,
        out_shape=pltpu.VMEM(wskip.shape, wskip.dtype),
        in_specs=[ANY, ANY],
        out_specs=VM,
        scratch_shapes=[pltpu.SemaphoreType.DMA(())],
        compiler_params=params(4),
        name="load_skip",
    )(in_hbm(wskip), after)


def skip_part(skip_in, wskip, first_section):
    width = skip_in.shape[1]

    def kernel(skip_ref, w_ref, out_ref):
        @pl.when(lax.axis_index("sec") >= first_section)
        def _():
            out_ref[...] = jnp.dot(skip_ref[...], w_ref[width:, :], preferred_element_type=jnp.float32)

    return pl.pallas_call(
        kernel,
        out_shape=jax.ShapeDtypeStruct(skip_in.shape, jnp.float32),
        in_specs=[VM, VM],
        out_specs=VM,
        compiler_params=params(8),
        name="skip_part",
    )(skip_in, wskip)


def enter_first(source, moment):
    def kernel(u_ref, normed_ref):
        @pl.when(lax.axis_index("sec") == moment)
        def _():
            normed_ref[...] = norm_rows(u_ref[...].astype(jnp.float32)).astype(jnp.bfloat16)

    normed = pl.pallas_call(
        kernel,
        out_shape=jax.ShapeDtypeStruct(source.shape, jnp.bfloat16),
        in_specs=[VM],
        out_specs=VM,
        compiler_params=params(8),
        name="enter_first",
    )(source)
    return source, normed


def enter_second(source, wskip, part, moment):
    width = source.shape[1]

    def kernel(*refs):
        u_ref, w_ref = refs[:2]
        resid_ref, normed_ref = refs[-2:]

        @pl.when(lax.axis_index("sec") == moment)
        def _():
            mixed = jnp.dot(u_ref[...], w_ref[:width, :], preferred_element_type=jnp.float32)
            if part is None:
                mixed += jnp.dot(u_ref[...], w_ref[width:, :], preferred_element_type=jnp.float32)
            else:
                mixed += refs[2][...]
            resid = norm_rows(mixed).astype(jnp.bfloat16)
            resid_ref[...] = resid
            normed_ref[...] = norm_rows(resid.astype(jnp.float32)).astype(jnp.bfloat16)

    operands = (source, wskip) if part is None else (source, wskip, part)
    return pl.pallas_call(
        kernel,
        out_shape=(jax.ShapeDtypeStruct(source.shape, jnp.bfloat16),) * 2,
        in_specs=[VM] * len(operands),
        out_specs=(VM, VM),
        compiler_params=params(8),
        name="enter_second",
    )(*operands)


def attend(own, other, stale, wqkv, wout, tables, bias, moment, patch_count):
    own_rows, model = own.shape
    rows = 2 * own_rows
    piece = own_rows // patch_count
    width = wqkv.shape[2]
    padded = tables.shape[2]
    tile = stale.shape[1]
    scale = math.log2(math.e) / math.sqrt(HEAD_DIM)

    def kernel(own_ref, oth_ref, kv_ref, w_ref, wo_ref, tab_ref, bias_ref, keep_ref, send_ref, x_ref, q_ref, k_ref, v_ref, a_ref):
        def head_window(buf_ref, base, start, low, span):
            lane = lax.broadcasted_iota(jnp.int32, (1, span), 1) + low
            inside = (lane >= start) & (lane < start + HEAD_DIM)
            at = pl.ds(low, span)
            raw = jnp.where(inside, buf_ref[:, at], 0.0)
            mean = jnp.sum(raw, axis=-1, keepdims=True) / HEAD_DIM
            centred = jnp.where(inside, raw - mean, 0.0)
            variance = jnp.sum(centred * centred, axis=-1, keepdims=True) / HEAD_DIM
            unit = centred * (1.0 / jnp.sqrt(variance + EPSILON))
            turned = (
                unit * tab_ref[base, :, at]
                + pltpu.roll(unit, span - HALF, 1) * tab_ref[base + 1, :, at]
                + pltpu.roll(unit, HALF, 1) * tab_ref[base + 2, :, at]
            )
            return jnp.where(inside, turned, 0.0).astype(jnp.bfloat16), inside

        @pl.when(lax.axis_index("sec") == moment)
        def _():
            for k in range(patch_count):
                x_ref[2 * k * piece : (2 * k + 1) * piece, :] = own_ref[k * piece : (k + 1) * piece, :]
                x_ref[(2 * k + 1) * piece : (2 * k + 2) * piece, :] = oth_ref[k * piece : (k + 1) * piece, :]
            q_ref[:, width:] = jnp.zeros((rows, padded - width), jnp.float32)
            k_ref[:, width:] = jnp.zeros((rows, padded - width), jnp.float32)
            q_ref[:, :width] = jnp.dot(x_ref[...], w_ref[0], preferred_element_type=jnp.float32)
            k_ref[:, :width] = jnp.dot(x_ref[...], w_ref[1], preferred_element_type=jnp.float32)
            v_ref[...] = jnp.dot(x_ref[...], w_ref[2], preferred_element_type=jnp.float32).astype(jnp.bfloat16)
            groups = [jnp.zeros((rows, LANES), jnp.float32) for _ in range(padded // LANES)]
            contract = (((1,), (1,)), ((), ()))
            for start, low, span in windows(width):
                query, inside = head_window(q_ref, 0, start, low, span)
                fresh, _ = head_window(k_ref, 3, start, low, span)
                real = min(span, width - low)
                at = pl.ds(low, real)
                old_scores = lax.dot_general(query[:, :real], kv_ref[0, :, at], contract, preferred_element_type=jnp.float32)
                new_scores = lax.dot_general(query, fresh, contract, preferred_element_type=jnp.float32)
                old = jnp.exp2(old_scores * scale + bias_ref[:, :tile])
                new = jnp.exp2(new_scores * scale + bias_ref[:, tile:])
                total = jnp.sum(old, axis=-1, keepdims=True) + jnp.sum(new, axis=-1, keepdims=True)
                mixed = jnp.dot(old.astype(jnp.bfloat16), kv_ref[1, :, at], preferred_element_type=jnp.float32)
                mixed += jnp.dot(new.astype(jnp.bfloat16), v_ref[:, at], preferred_element_type=jnp.float32)
                mixed = mixed / total
                if real < span:
                    mixed = jnp.concatenate([mixed, jnp.zeros((rows, span - real), jnp.float32)], axis=1)
                for part in range(span // LANES):
                    piece_at = slice(part * LANES, (part + 1) * LANES)
                    group = low // LANES + part
                    groups[group] = jnp.where(inside[:, piece_at], mixed[:, piece_at], groups[group])
            for group, value in enumerate(groups):
                last = min(LANES, width - group * LANES)
                a_ref[:, group * LANES : group * LANES + last] = value[:, :last].astype(jnp.bfloat16)
            partial = jnp.dot(a_ref[...], wo_ref[...], preferred_element_type=jnp.float32)
            for k in range(patch_count):
                at = slice(k * piece, (k + 1) * piece)
                keep_ref[at, :] = partial[2 * k * piece : (2 * k + 1) * piece]
                send_ref[at, :] = partial[(2 * k + 1) * piece : (2 * k + 2) * piece].astype(jnp.bfloat16)

    return pl.pallas_call(
        kernel,
        out_shape=(
            jax.ShapeDtypeStruct(own.shape, jnp.float32),
            jax.ShapeDtypeStruct(own.shape, jnp.bfloat16),
        ),
        in_specs=[VM] * 7,
        out_specs=(VM, VM),
        scratch_shapes=[
            pltpu.VMEM((rows, model), jnp.bfloat16),
            pltpu.VMEM((rows, padded), jnp.float32),
            pltpu.VMEM((rows, padded), jnp.float32),
            pltpu.VMEM((rows, width), jnp.bfloat16),
            pltpu.VMEM((rows, width), jnp.bfloat16),
        ],
        compiler_params=params(16),
        name="attend",
    )(own, other, stale, wqkv, wout, tables, bias)


def leave(resid, keep, arrived, mine, moment):
    def kernel(resid_ref, keep_ref, arrived_ref, mine_ref, out_ref):
        @pl.when(lax.axis_index("sec") == moment)
        def _():
            total = keep_ref[...] + arrived_ref[...].astype(jnp.float32)
            out_ref[...] = (resid_ref[...].astype(jnp.float32) + total).astype(jnp.bfloat16)

    return pl.pallas_call(
        kernel,
        out_shape=jax.ShapeDtypeStruct(mine.shape, mine.dtype),
        in_specs=[VM] * 4,
        out_specs=VM,
        input_output_aliases={3: 0},
        compiler_params=params(8),
        name="leave",
    )(resid, keep, arrived, mine)


def body(patches, stale_kv, qkv_weight, out_weight, skip_joined_weight, qk_gain, order, tile_index):
    patch_count, piece, model = patches.shape
    own_rows = patch_count * piece
    patch_rows = 2 * piece
    tile = stale_kv.shape[2]
    width = stale_kv.shape[3]
    padded = -(-width // LANES) * LANES
    sections = lax.axis_size("sec")
    half = sections // 2
    head = lax.axis_index("head")
    swap = [(0, 1), (1, 0)]

    local = jnp.arange(piece, dtype=jnp.int32)
    in_patch = jnp.concatenate([head * piece + local, (1 - head) * piece + local])
    slots = order[:patch_count]
    flat = tile_index[0] * tile + slots[:, None] * patch_rows + in_patch[None, :]
    position = flat.reshape(-1).astype(jnp.float32)
    index = jnp.arange(LANES, dtype=jnp.int32) % HALF
    inverse = 10000.0 ** (-index.astype(jnp.float32) / HALF)
    angles = position[:, None] * inverse[None, :]
    cosine = jnp.cos(angles)
    sine = jnp.sin(angles)
    gains = jnp.pad(qk_gain[0].astype(jnp.float32), ((0, 0), (0, padded - width)))
    row_patch = jnp.arange(patch_count * patch_rows, dtype=jnp.int32) // patch_rows
    column = jnp.arange(tile, dtype=jnp.int32) // patch_rows
    hidden_old = jnp.zeros((patch_count * patch_rows, tile), bool)
    for k in range(patch_count):
        hidden_old |= (column[None, :] == slots[k]) & (row_patch[:, None] >= k)
    hidden_new = row_patch[None, :] > row_patch[:, None]
    bias = jnp.where(jnp.concatenate([hidden_old, hidden_new], axis=1), MASKED, 0.0).astype(jnp.float32)

    stale, wqkv, wout, tables = load_first(
        stale_kv[0], qkv_weight[0], out_weight[0], cosine, sine, gains
    )
    wskip = None
    part = None
    source = patches.reshape(own_rows, model)
    mine = jnp.zeros((own_rows, model), jnp.bfloat16)
    for moment in range(sections):
        if moment < half:
            resid, normed = enter_first(source, moment)
        else:
            resid, normed = enter_second(source, wskip, None if moment == half else part, moment)
        other = lax.ppermute(normed, "head", swap)
        keep, send = attend(normed, other, stale, wqkv, wout, tables, bias, moment, patch_count)
        if moment == 0:
            wskip = load_skip(skip_joined_weight[0], send)
        arrived = lax.ppermute(send, "head", swap)
        mine = leave(resid, keep, arrived, mine, moment)
        if moment < sections - 1:
            source = lax.ppermute(mine, "sec", [(moment, moment + 1)])
        if moment == half - 2:
            pairs = [(i, sections - 1 - i) for i in range(half - 1)]
            skip_in = lax.ppermute(mine, "sec", pairs)
            part = skip_part(skip_in, wskip, half + 1)
    return mine.reshape(1, patch_count, piece, model)


def solution(mesh):
    return jax.shard_map(
        body,
        mesh=mesh,
        in_specs=(
            P("grp", "head", None),
            P(("grp", "sec"), None, None, "head"),
            P("sec", None, None, "head"),
            P("sec", "head", None),
            P("sec", None, None),
            P("sec", None, "head"),
            P("grp"),
            P("grp"),
        ),
        out_specs=P("sec", "grp", "head", None),
        check_vma=False,
    )
```

```python
import math

import jax
import jax.numpy as jnp
from jax import lax
from jax.experimental import pallas as pl
from jax.experimental.pallas import tpu as pltpu
from jax.sharding import PartitionSpec as P

HEAD_DIM = 88
HALF = HEAD_DIM // 2
LANES = 128
ONES = 8
EPSILON = 1e-06

VM = pl.BlockSpec(memory_space=pltpu.VMEM)
SM = pl.BlockSpec(memory_space=pltpu.SMEM)
ANY = pl.BlockSpec(memory_space=pl.ANY)


def norm_rows(value):
    mean = jnp.mean(value, axis=-1, keepdims=True)
    centred = value - mean
    variance = jnp.mean(centred * centred, axis=-1, keepdims=True)
    return centred / jnp.sqrt(variance + EPSILON)


def params(mib):
    return pltpu.CompilerParams(vmem_limit_bytes=mib << 20)


def in_hbm(value):
    return pltpu.with_memory_space_constraint(value, pltpu.HBM)


def load_first(stale, wqkv, wout, gains, order, tile_index, patch_count, piece):
    heads, tile = stale.shape[1], stale.shape[3]

    def kernel(order_ref, tile_ref, gain_ref, kv_ref, w_ref, o_ref, k_out, v_out, w_out, o_out, tab_out, sems):
        copies = [
            pltpu.make_async_copy(w_ref, w_out, sems.at[0]),
            pltpu.make_async_copy(kv_ref.at[0], k_out, sems.at[1]),
            pltpu.make_async_copy(kv_ref.at[1], v_out.at[:, :HEAD_DIM, :], sems.at[2]),
            pltpu.make_async_copy(o_ref, o_out, sems.at[3]),
        ]
        for copy in copies:
            copy.start()
        v_out[:, HEAD_DIM:, :] = jnp.ones((heads, ONES, tile), jnp.bfloat16)
        head = lax.axis_index("head")
        lane = lax.broadcasted_iota(jnp.int32, (HEAD_DIM, LANES), 1)
        row = lax.broadcasted_iota(jnp.int32, (HEAD_DIM, LANES), 0)
        local = jnp.where(lane >= 2 * piece, lane - 2 * piece, lane)
        in_patch = jnp.where(local < piece, head * piece + local, (1 - head) * piece + local - piece)
        index = jnp.where(row >= HALF, row - HALF, row).astype(jnp.float32)
        inverse = jnp.exp(index * (-math.log(10000.0) / HALF))
        for k in range(patch_count):
            slot = order_ref[k]
            base = tile_ref[0] * tile + slot * (2 * piece)
            angle = (base + in_patch).astype(jnp.float32) * inverse
            cosine = jnp.cos(angle)
            sine = jnp.sin(angle)
            sine = jnp.where(row < HALF, -sine, sine)
            of_keys = (lane >= 2 * piece) == (slot % 2 == 1)
            for h in range(heads):
                gain = jnp.where(of_keys, gain_ref[1, h], gain_ref[0, h])
                tab_out[k, 0, h] = cosine * gain
                tab_out[k, 1, h] = sine * pltpu.roll(gain, HALF, 0)
        for copy in copies:
            copy.wait()

    return pl.pallas_call(
        kernel,
        out_shape=(
            pltpu.VMEM((heads, HEAD_DIM, tile), stale.dtype),
            pltpu.VMEM((heads, HEAD_DIM + ONES, tile), stale.dtype),
            pltpu.VMEM(wqkv.shape, wqkv.dtype),
            pltpu.VMEM(wout.shape, wout.dtype),
            pltpu.VMEM((patch_count, 2, heads, HEAD_DIM, LANES), jnp.float32),
        ),
        in_specs=[SM, SM, VM, ANY, ANY, ANY],
        out_specs=(VM,) * 5,
        scratch_shapes=[pltpu.SemaphoreType.DMA((4,))],
        compiler_params=params(8),
        name="load_first",
    )(order, tile_index, gains, in_hbm(stale), in_hbm(wqkv), in_hbm(wout))


def load_skip(wskip, after, half):
    def kernel(w_ref, after_ref, w_out, sem):
        @pl.when(lax.axis_index("sec") >= half)
        def _():
            copy = pltpu.make_async_copy(w_ref, w_out, sem)
            copy.start()
            copy.wait()

    return pl.pallas_call(
        kernel,
        out_shape=pltpu.VMEM(wskip.shape, wskip.dtype),
        in_specs=[ANY, ANY],
        out_specs=VM,
        scratch_shapes=[pltpu.SemaphoreType.DMA(())],
        compiler_params=params(4),
        name="load_skip",
    )(in_hbm(wskip), after)


def skip_part(skip_in, wskip, first_section):
    count, rows, width = skip_in.shape

    def kernel(skip_ref, w_ref, out_ref):
        @pl.when(lax.axis_index("sec") >= first_section)
        def _():
            flat = skip_ref[...].reshape(count * rows, width)
            product = jnp.dot(flat, w_ref[width:, :], preferred_element_type=jnp.float32)
            out_ref[...] = product.reshape(count, rows, width)

    return pl.pallas_call(
        kernel,
        out_shape=jax.ShapeDtypeStruct(skip_in.shape, jnp.float32),
        in_specs=[VM, VM],
        out_specs=VM,
        compiler_params=params(8),
        name="skip_part",
    )(skip_in, wskip)


def enter_first(source, after, moment):
    def kernel(u_ref, after_ref, normed_ref):
        @pl.when(lax.axis_index("sec") == moment)
        def _():
            normed_ref[...] = norm_rows(u_ref[...].astype(jnp.float32)).astype(jnp.bfloat16)

    normed = pl.pallas_call(
        kernel,
        out_shape=jax.ShapeDtypeStruct(source.shape, jnp.bfloat16),
        in_specs=[VM, ANY],
        out_specs=VM,
        compiler_params=params(8),
        name="enter_first",
    )(source, after)
    return source, normed


def enter_second(source, wskip, part, after, moment, patch):
    width = source.shape[1]

    def kernel(*refs):
        u_ref, w_ref = refs[:2]
        resid_ref, normed_ref = refs[-2:]

        @pl.when(lax.axis_index("sec") == moment)
        def _():
            mixed = jnp.dot(u_ref[...], w_ref[:width, :], preferred_element_type=jnp.float32)
            if part is None:
                mixed += jnp.dot(u_ref[...], w_ref[width:, :], preferred_element_type=jnp.float32)
            else:
                mixed += refs[3][patch]
            resid = norm_rows(mixed).astype(jnp.bfloat16)
            resid_ref[...] = resid
            normed_ref[...] = norm_rows(resid.astype(jnp.float32)).astype(jnp.bfloat16)

    operands = (source, wskip, after) if part is None else (source, wskip, after, part)
    return pl.pallas_call(
        kernel,
        out_shape=(jax.ShapeDtypeStruct(source.shape, jnp.bfloat16),) * 2,
        in_specs=[VM, VM, ANY, VM][: len(operands)],
        out_specs=(VM, VM),
        compiler_params=params(8),
        name="enter_second",
    )(*operands)


def attend(own, other, keys, values, wqkv, wout, tables, order, moment, patch):
    piece, model = own.shape
    rows = 2 * piece
    heads, _, tile = keys.shape
    width = heads * HEAD_DIM
    scale = math.log2(math.e) / math.sqrt(HEAD_DIM)
    by_lanes = (((1,), (1,)), ((), ()))

    def kernel(own_ref, oth_ref, w_ref, wo_ref, tab_ref, order_ref, k_in, v_in, keep_ref, send_ref, k_ref, v_ref, xk_ref, xq_ref, qk_ref, vn_ref, q_ref, a_ref):
        @pl.when(lax.axis_index("sec") == moment)
        def _():
            slot = order_ref[patch]
            odd = slot % 2
            of_keys = pl.multiple_of(odd * rows, rows)
            of_query = pl.multiple_of((1 - odd) * rows, rows)
            group = pl.ds(pl.multiple_of(slot // 2 * LANES, LANES), LANES)
            blank = jnp.zeros((rows, model), jnp.bfloat16)
            xk_ref[pl.ds(of_query, rows), :] = blank
            xq_ref[pl.ds(of_keys, rows), :] = blank
            for ref, start in ((xk_ref, of_keys), (xq_ref, of_query)):
                ref[pl.ds(start, piece), :] = own_ref[...]
                ref[pl.ds(pl.multiple_of(start + piece, piece), piece), :] = oth_ref[...]
            product = lax.dot_general(w_ref[0], xq_ref[...], by_lanes, preferred_element_type=jnp.float32)
            product += lax.dot_general(w_ref[1], xk_ref[...], by_lanes, preferred_element_type=jnp.float32)
            qk_ref[...] = product.reshape(heads, HEAD_DIM, LANES)
            fresh = lax.dot_general(w_ref[2], xk_ref[...], by_lanes, preferred_element_type=jnp.float32)
            vn_ref[...] = fresh.reshape(heads, HEAD_DIM, LANES)
            mine = (lax.broadcasted_iota(jnp.int32, (HEAD_DIM, LANES), 1) >= rows) == (odd == 1)

            def prepare(h, _):
                raw = qk_ref[h]
                centred = raw - jnp.mean(raw, axis=0, keepdims=True)
                variance = jnp.mean(centred * centred, axis=0, keepdims=True)
                unit = centred * (1.0 / jnp.sqrt(variance + EPSILON))
                turned = unit * tab_ref[patch, 0, h] + pltpu.roll(unit, HALF, 0) * tab_ref[patch, 1, h]
                k_ref[h, :, group] = jnp.where(mine, turned, k_ref[h, :, group].astype(jnp.float32)).astype(jnp.bfloat16)
                old = v_ref[h, :HEAD_DIM, group].astype(jnp.float32)
                v_ref[h, :HEAD_DIM, group] = jnp.where(mine, vn_ref[h], old).astype(jnp.bfloat16)
                q_ref[h] = turned.T.astype(jnp.bfloat16)
                return 0

            lax.fori_loop(0, heads, prepare, 0, unroll=True)

            def mix(h, _):
                query = q_ref[h, pl.ds(of_query, rows), :]
                scores = jnp.dot(query, k_ref[h], preferred_element_type=jnp.float32)
                weights = jnp.exp2(scores * scale).astype(jnp.bfloat16)
                mixed = lax.dot_general(v_ref[h], weights, by_lanes, preferred_element_type=jnp.float32)
                a_ref[h] = mixed[:HEAD_DIM] / mixed[HEAD_DIM : HEAD_DIM + 1]
                return 0

            lax.fori_loop(0, heads, mix, 0, unroll=True)
            attended = a_ref[...].reshape(width, rows).T.astype(jnp.bfloat16)
            partial = jnp.dot(attended, wo_ref[...], preferred_element_type=jnp.float32)
            keep_ref[...] = partial[:piece]
            send_ref[...] = partial[piece:].astype(jnp.bfloat16)

    return pl.pallas_call(
        kernel,
        out_shape=(
            jax.ShapeDtypeStruct(own.shape, jnp.float32),
            jax.ShapeDtypeStruct(own.shape, jnp.bfloat16),
            pltpu.VMEM(keys.shape, keys.dtype),
            pltpu.VMEM(values.shape, values.dtype),
        ),
        in_specs=[VM, VM, VM, VM, VM, SM, VM, VM],
        out_specs=(VM,) * 4,
        input_output_aliases={6: 2, 7: 3},
        scratch_shapes=[
            pltpu.VMEM((LANES, model), jnp.bfloat16),
            pltpu.VMEM((LANES, model), jnp.bfloat16),
            pltpu.VMEM((heads, HEAD_DIM, LANES), jnp.float32),
            pltpu.VMEM((heads, HEAD_DIM, LANES), jnp.float32),
            pltpu.VMEM((heads, LANES, HEAD_DIM), jnp.bfloat16),
            pltpu.VMEM((heads, HEAD_DIM, rows), jnp.float32),
        ],
        compiler_params=params(12),
        name="attend",
    )(own, other, wqkv, wout, tables, order, keys, values)


def leave(resid, keep, arrived, mine, moment):
    def kernel(resid_ref, keep_ref, arrived_ref, mine_ref, out_ref):
        @pl.when(lax.axis_index("sec") == moment)
        def _():
            total = keep_ref[...] + arrived_ref[...].astype(jnp.float32)
            out_ref[...] = (resid_ref[...].astype(jnp.float32) + total).astype(jnp.bfloat16)

        @pl.when(lax.axis_index("sec") != moment)
        def _():
            out_ref[...] = mine_ref[...]

    return pl.pallas_call(
        kernel,
        out_shape=pltpu.VMEM(mine.shape, mine.dtype),
        in_specs=[VM] * 4,
        out_specs=VM,
        compiler_params=params(8),
        name="leave",
    )(resid, keep, arrived, mine)


def body(patches, stale_kv, qkv_weight, out_weight, skip_joined_weight, qk_gain, order, tile_index):
    patch_count, piece, model = patches.shape
    tile, width = stale_kv.shape[2:]
    heads = width // HEAD_DIM
    sections = lax.axis_size("sec")
    half = sections // 2
    swap = [(0, 1), (1, 0)]

    stale = jnp.swapaxes(stale_kv[0], 1, 2).reshape(2, heads, HEAD_DIM, tile)
    wqkv = jnp.swapaxes(qkv_weight[0], 1, 2)
    gains = jnp.broadcast_to(
        qk_gain[0].astype(jnp.float32).reshape(2, heads, HEAD_DIM, 1), (2, heads, HEAD_DIM, LANES)
    )
    keys, values, wqkv, wout, tables = load_first(
        stale, wqkv, out_weight[0], gains, order, tile_index, patch_count, piece
    )
    wskip = load_skip(skip_joined_weight[0], tables, half)
    part = None
    after = patches
    source = [patches[k] for k in range(patch_count)]
    mine = [patches[k] for k in range(patch_count)]
    for moment in range(sections + patch_count - 1):
        for k in reversed(range(patch_count)):
            section = moment - k
            if section < 0 or section >= sections:
                continue
            if section < half:
                resid, normed = enter_first(source[k], after, section)
            else:
                ready = None if section == half else part
                resid, normed = enter_second(source[k], wskip, ready, after, section, k)
            other = lax.ppermute(normed, "head", swap)
            keep, send, keys, values = attend(
                normed, other, keys, values, wqkv, wout, tables, order, section, k
            )
            arrived = lax.ppermute(send, "head", swap)
            mine[k] = leave(resid, keep, arrived, mine[k], section)
            after = mine[k]
            if section < sections - 1:
                source[k] = lax.ppermute(mine[k], "sec", [(section, section + 1)])
            if section == half - 2 and k == patch_count - 1:
                pairs = [(i, sections - 1 - i) for i in range(half - 1)]
                skip_in = lax.ppermute(jnp.stack(mine), "sec", pairs)
                part = skip_part(skip_in, wskip, half + 1)
    return jnp.stack(mine)[None]


def solution(mesh):
    return jax.shard_map(
        body,
        mesh=mesh,
        in_specs=(
            P("grp", "head", None),
            P(("grp", "sec"), None, None, "head"),
            P("sec", None, None, "head"),
            P("sec", "head", None),
            P("sec", None, None),
            P("sec", None, "head"),
            P("grp"),
            P("grp"),
        ),
        out_specs=P("sec", "grp", "head", None),
        check_vma=False,
    )
```
